32 devices in a mesh: dp: 2 (over x), expert: 16 (over z, y, core).
Axes of the slice: x: 2, y: 2, z: 4, core: 2. Of those that a mesh axis runs over, the one named last changes fastest.
Arguments:
- query_nope: bfloat16 [16, 128, 2048], P('expert', None, 'dp'), may hold values from -6 to 6
- query_rope: bfloat16 [16, 128, 1024], P('expert', None, 'dp'), may hold values from -8 to 8
- latent_new: bfloat16 [16, 128, 512], P('expert'), may hold values from -6 to 6
- key_rope: bfloat16 [16, 128, 64], P('expert'), may hold values from -8 to 8
- latent_pages: bfloat16 [16, 8, 64, 512], P('expert', 'dp'), may hold values from -6 to 6
- rope_pages: bfloat16 [16, 8, 4096], P('expert', 'dp'), may hold values from -6 to 6
- page_table: int32 [16, 8], P('expert'), may hold values from 0 to 7, each once within a row
- prefix_lengths: int32 [16], P('expert'), may hold values from 0 to 512, as said below
- residual: bfloat16 [16, 128, 2048], P('expert'), may hold values from -60 to 60
- key_up: bfloat16 [16, 128, 512], P('dp'), may hold values from -0.5 to 0.5
- value_up: bfloat16 [16, 512, 128], P('dp'), may hold values from -0.25 to 0.25
- out_weight: bfloat16 [2048, 2048], P('dp'), may hold values from -0.125 to 0.125
- norm_gain: float32 [2048], replicated, may hold values from 0.1 to 1.9
- expert_in: bfloat16 [16, 1408, 2, 2048], P('expert', 'dp'), may hold values from -0.125 to 0.125
- expert_down: bfloat16 [16, 1408, 2048], P('expert', 'dp'), may hold values from -0.15625 to 0.15625
- expert_ids: int32 [16, 128, 6], P('expert'), may hold values from 0 to 15, all different within a row; in each aligned block of 64 rows (0 to 63, 64 to 127, ..., all dimensions but the last counted through in order) at most 48 rows name the same one
- expert_weights: float32 [16, 128, 6], P('expert'), may hold values from 0.05 to 0.4
Outputs:
- layer_out: bfloat16 [16, 128, 2048], P('expert', 'dp')
- expert_mix: bfloat16 [16, 128, 2048], P('expert', 'dp')
The draws below stay inside these ranges and needn't reach their ends.
Inputs may be any that keep to these rules, and one draw needn't show every extreme that they name: `prefix_lengths`: some request's prefix fills all of its 8 page slots. `page_table`: each row names every page slot of its request once; entry j holds positions j * 64 to (j + 1) * 64 - 1. `expert_ids`: each row names 6 distinct experts; in each aligned block of 64 rows of a request (blocks along the first two dimensions taken together) no expert is named more than 48 times, and that many is reached.
All inputs are finite; a program needn't handle non-finite values.
Results may differ from the reference program's by a relative error of at most 0.019.
Values may be sent and summed in bfloat16 or wider, within the bound.
A program may use at most 128 MiB of HBM per device.

```python
import math
import jax
import jax.numpy as jnp
import numpy as np
from jax import lax

D = 2048
H = 16
HD = 128
RD = 64
LAT = 512
FFE = 1408
TOP = 6
PAGE = 64
T_COL = 128
EXPERTS = 16
REQS = 16
PAGES = 8
HSPLIT = 2
QROWS = 64
CAPQ = 48


def rope_pair(key):
    base_k = jnp.clip(jax.random.normal(jax.random.fold_in(key, 11), (REQS, T_COL, RD), jnp.float32), -6.0, 6.0)
    base_q = jnp.clip(jax.random.normal(jax.random.fold_in(key, 12), (REQS, T_COL, H * RD), jnp.float32), -6.0, 6.0)
    return (base_q, base_k)


def draw_query_rope(key, part):
    return rope_pair(key)[0].astype(jnp.bfloat16)


def draw_key_rope(key, part):
    return rope_pair(key)[1].astype(jnp.bfloat16)


def draw_residual(key, part):
    low = math.log(0.3)
    high = math.log(3.0)
    row_scale = jnp.exp(jax.random.uniform(jax.random.fold_in(key, 31), (REQS, T_COL, 1), jnp.float32, low, high))
    col_scale = jnp.exp(jax.random.uniform(jax.random.fold_in(key, 32), (1, 1, D), jnp.float32, low, high))
    base = jnp.clip(jax.random.normal(jax.random.fold_in(key, 33), (REQS, T_COL, D), jnp.float32), -5.0, 5.0)
    return (base * row_scale * col_scale).astype(jnp.bfloat16)


def draw_prefix_lengths(key, part):
    lengths = jax.random.randint(jax.random.fold_in(key, 21), (REQS,), 0, PAGES * PAGE + 1)
    full = jax.random.randint(jax.random.fold_in(key, 22), (), 0, REQS)
    return jnp.where(jnp.arange(REQS) == full, PAGES * PAGE, lengths).astype(jnp.int32)


def block_levels(key, extent, split, low, high):
    loudness = 1.0
    for dim, shards_of in split:
        draws = jax.random.uniform(jax.random.fold_in(jax.random.fold_in(key, 6), dim), (shards_of,), jnp.float32, low / len(split), high / len(split))
        loudness = loudness * jnp.repeat(jnp.exp(draws), extent[dim] // shards_of).reshape((-1,) + (1,) * (len(extent) - 1 - dim))
    return loudness


def deal_out(stream_key, own, number, rows, count, top, most, slope):
    sequence = jax.random.permutation(stream_key, count)
    crowded, usual = load_shares(count, rows * top, most, slope, True), load_shares(count, rows * top, most, slope, False)
    places = jnp.arange(count)

    def named(tallies, rotation):
        used = int((tallies > 0).sum())
        fixed = max(1, used // 4)
        moved = fixed + (places - fixed + rotation * (used - fixed)) % max(1, count - fixed)
        return jnp.zeros((count,), jnp.int32).at[sequence[jnp.where(places < fixed, places, moved)]].set(jnp.asarray(tallies, jnp.int32))

    tallies = jnp.where(number % 4 == 0, named(crowded, number // 4), named(usual, number - number // 4 - 1))
    mixed = jax.random.permutation(jax.random.fold_in(own, 3), count)
    giver, taker = mixed[0:count // 2 * 2:2], mixed[1:count // 2 * 2:2]
    room = jnp.minimum(tallies[giver] - 1, most - tallies[taker]) // 2
    room = jnp.where((giver == sequence[0]) | (taker == sequence[0]) | (tallies[taker] == 0), 0, jnp.maximum(room, 0))
    moved = jax.random.randint(jax.random.fold_in(own, 4), (count // 2,), 0, 1 << 20) % (room + 1)
    tallies = tallies.at[giver].add(-moved).at[taker].add(moved)
    members = jnp.searchsorted(jnp.cumsum(tallies), jnp.arange(rows * top), side="right").astype(jnp.int32)
    grid = members.reshape(top, rows).T
    grid = grid[jax.random.permutation(jax.random.fold_in(own, 1), rows)]
    rotation = jax.random.randint(jax.random.fold_in(own, 2), (rows, 1), 0, top)
    return jnp.take_along_axis(grid, (jnp.arange(top)[None, :] + rotation) % top, axis=1)


def load_shares(count, total, bound, slope, full):
    loads = [(1 << 20) // math.isqrt(grade ** slope) + 1 for grade in range(1, count + 1)]
    largest = bound if full else min(bound, max(-(-total // count), total * loads[0] // sum(loads)))
    least = 1 if total - largest >= count - 1 else 0
    counts, surplus = [largest] + [least] * (count - 1), total - largest - least * (count - 1)
    while surplus > 0:
        free = [i for i in range(1, count) if counts[i] < largest] or [i for i in range(1, count) if counts[i] < bound]
        whole, budget = sum([loads[i] for i in free]), surplus
        for i in free:
            addition = min(bound - counts[i], max(1, budget * loads[i] // whole), surplus)
            counts[i] = counts[i] + addition
            surplus = surplus - addition
    return np.array(counts)


def scatter_about(key, dims, spread, bound, pieces=(), held_as=jnp.bfloat16):
    array = jax.random.normal(key, dims, jnp.float32) * spread
    if len(pieces) > 0:
        array = block_levels(key, dims, pieces, -0.22, 0.18) * array
    return jnp.clip(array, min=-bound, max=bound).astype(held_as)


def setup_inputs(seed: int = 0) -> dict:
    streams_of = jax.random.split(jax.random.key(seed), 18)
    query_nope = scatter_about(streams_of[0], (REQS, T_COL, H * HD), 1.0, 6.0, ((0, 16), (2, 2)))
    query_rope = draw_query_rope(jax.random.fold_in(streams_of[17], 71), 0)
    latent_new = scatter_about(streams_of[2], (REQS, T_COL, LAT), 1.0, 6.0, ((0, 16),))
    key_rope = draw_key_rope(jax.random.fold_in(streams_of[17], 71), 0)
    latent_pages = scatter_about(streams_of[4], (REQS, PAGES, PAGE, LAT), 1.0, 6.0, ((0, 16), (1, 2)))
    rope_pages = scatter_about(streams_of[5], (REQS, PAGES, PAGE * RD), 1.0, 6.0, ((0, 16), (1, 2)))
    page_table = jax.vmap(lambda own: jax.random.permutation(own, PAGES))(jax.random.split(streams_of[6], REQS)).reshape((REQS, PAGES)).astype(jnp.int32)
    prefix_lengths = draw_prefix_lengths(jax.random.fold_in(streams_of[17], 71), 0)
    residual = draw_residual(jax.random.fold_in(streams_of[17], 71), 0)
    key_up = scatter_about(streams_of[9], (H, HD, LAT), HD ** -0.5, 0.5, ((0, 2),))
    value_up = scatter_about(streams_of[10], (H, LAT, HD), LAT ** -0.5, 0.25, ((0, 2),))
    out_weight = scatter_about(streams_of[11], (H * HD, D), (H * HD) ** -0.5, 0.125, ((0, 2),))
    norm_gain = jnp.clip(1.0 + 0.18 * jax.random.normal(streams_of[12], (D,), jnp.float32), 0.1, 1.9)
    expert_in = scatter_about(streams_of[13], (EXPERTS, FFE, 2, D), D ** -0.5, 0.125, ((0, 16), (1, 2)))
    expert_down = scatter_about(streams_of[14], (EXPERTS, FFE, D), FFE ** -0.5, 0.15625, ((0, 16), (1, 2)))
    expert_ids_keys = jax.random.split(jax.random.fold_in(streams_of[15], 1), REQS * T_COL // QROWS)
    expert_ids_turns = jax.random.permutation(jax.random.fold_in(streams_of[15], 3), REQS * T_COL // QROWS)
    expert_ids = jax.vmap(lambda own, number: deal_out(jax.random.fold_in(streams_of[15], 2), own, number, QROWS, EXPERTS, TOP, CAPQ, 2))(expert_ids_keys, expert_ids_turns).reshape((REQS, T_COL, TOP))
    expert_weights = jnp.clip(0.05 + 0.35 * jax.random.uniform(streams_of[16], (REQS, T_COL, TOP), jnp.float32) ** block_levels(streams_of[16], (REQS, T_COL, TOP), ((0, 16),), -0.2, 0.2), 0.05, 0.4)
    return {"query_nope": query_nope, "query_rope": query_rope, "latent_new": latent_new, "key_rope": key_rope, "latent_pages": latent_pages, "rope_pages": rope_pages, "page_table": page_table, "prefix_lengths": prefix_lengths, "residual": residual, "key_up": key_up, "value_up": value_up, "out_weight": out_weight, "norm_gain": norm_gain, "expert_in": expert_in, "expert_down": expert_down, "expert_ids": expert_ids, "expert_weights": expert_weights}


EPS = 1e-06
NEG = -1e+30

def rounded(value):
    return lax.optimization_barrier(value.astype(jnp.bfloat16)).astype(jnp.float32)

def reference(query_nope, query_rope, latent_new, key_rope, latent_pages, rope_pages, page_table, prefix_lengths, residual, key_up, value_up, out_weight, norm_gain, expert_in, expert_down, expert_ids, expert_weights):
    scale = 1.0 / (HD + RD) ** 0.5
    key_up_f = key_up.astype(jnp.float32)
    value_up_f = value_up.astype(jnp.float32)

    def attend(items):
        nope_rows, rope_rows, latent_rows, krope_rows, page_lat, page_rope, table, length, resid_rows = items
        heads_nope = nope_rows.reshape(T_COL, H, HD).astype(jnp.float32)
        query_lat = rounded(jnp.einsum('thd,hdc->thc', heads_nope, key_up_f))
        ordered_lat = page_lat[table].reshape(PAGES * PAGE, LAT)
        ordered_rope = page_rope[table].reshape(PAGES * PAGE, RD)
        keys_lat = jnp.concatenate([ordered_lat, latent_rows], axis=0).astype(jnp.float32)
        keys_rope = jnp.concatenate([ordered_rope, krope_rows], axis=0).astype(jnp.float32)
        heads_rope = rope_rows.reshape(T_COL, H, RD).astype(jnp.float32)
        scores = (jnp.einsum('thc,kc->thk', query_lat, keys_lat) + jnp.einsum('thr,kr->thk', heads_rope, keys_rope)) * scale
        prefix_ok = jnp.arange(PAGES * PAGE) < length
        causal = jnp.arange(T_COL)[None, :] <= jnp.arange(T_COL)[:, None]
        allowed = jnp.concatenate([jnp.broadcast_to(prefix_ok[None, :], (T_COL, PAGES * PAGE)), causal], axis=1)[:, None, :]
        masked = jnp.where(allowed, scores, NEG)
        peak = lax.optimization_barrier(jnp.max(masked, axis=-1, keepdims=True))
        expo = jnp.where(allowed, jnp.exp(masked - peak), 0.0)
        total = lax.optimization_barrier(jnp.sum(expo, axis=-1, keepdims=True))
        probs = rounded(expo)
        attn_latent = rounded(jnp.einsum('thk,kc->thc', probs, keys_lat) / total)
        heads_out = jnp.einsum('thc,hcd->thd', attn_latent, value_up_f).astype(jnp.bfloat16)
        attn = jnp.dot(heads_out.reshape(T_COL, H * HD), out_weight, preferred_element_type=jnp.float32)
        return resid_rows.astype(jnp.float32) + attn
    hidden = lax.map(attend, (query_nope, query_rope, latent_new, key_rope, latent_pages, rope_pages, page_table, prefix_lengths, residual))
    rows = REQS * T_COL
    flat_hidden = hidden.reshape(rows, D)
    power = lax.optimization_barrier(jnp.mean(flat_hidden * flat_hidden, axis=-1, keepdims=True))
    normed = (flat_hidden * lax.rsqrt(power + EPS) * norm_gain).astype(jnp.bfloat16)
    flat_ids = expert_ids.reshape(rows * TOP)
    flat_gates = expert_weights.reshape(rows * TOP)
    onehot = (flat_ids[:, None] == jnp.arange(EXPERTS)[None, :]).astype(jnp.int32)
    before = jnp.cumsum(onehot, axis=0) - onehot
    rank = lax.optimization_barrier(jnp.sum(before * onehot, axis=1)).astype(jnp.int32)
    capacity = REQS * HSPLIT * CAPQ
    group_width = FFE // HSPLIT
    source_row = (jnp.arange(rows * TOP) // TOP).astype(jnp.int32)

    def add_expert(mixture, expert):
        chosen = flat_ids == expert
        slot = jnp.where(chosen, rank, capacity).astype(jnp.int32)
        row_of = jnp.zeros((capacity,), jnp.int32).at[slot].set(source_row, mode='drop')
        gate_of = jnp.zeros((capacity,), jnp.float32).at[slot].set(flat_gates, mode='drop')
        picked = normed[row_of]
        rows_in = expert_in[expert]
        rows_down = expert_down[expert]
        result = jnp.zeros((capacity, D), jnp.float32)
        for group in range(HSPLIT):
            lower = group * group_width
            upper = lower + group_width
            gate_act = jnp.dot(picked, rows_in[lower:upper, 0, :].T, preferred_element_type=jnp.float32)
            up_act = jnp.dot(picked, rows_in[lower:upper, 1, :].T, preferred_element_type=jnp.float32)
            units = (jax.nn.silu(gate_act) * up_act).astype(jnp.bfloat16)
            part = jnp.dot(units, rows_down[lower:upper], preferred_element_type=jnp.float32).astype(jnp.bfloat16)
            result = result + part.astype(jnp.float32)
        mixture = mixture.at[row_of].add(result * gate_of[:, None])
        return (mixture, None)
    mixture, unused = lax.scan(add_expert, jnp.zeros((rows, D), jnp.float32), jnp.arange(EXPERTS))
    layer_out = (flat_hidden + mixture).astype(jnp.bfloat16).reshape(REQS, T_COL, D)
    expert_mix = mixture.astype(jnp.bfloat16).reshape(REQS, T_COL, D)
    return (layer_out, expert_mix)
```

```python
import jax
import jax.numpy as jnp
from jax import lax
from jax.sharding import PartitionSpec as P

HD = 128
RD = 64
LAT = 512
TOP = 6
PAGE = 64


EPS = 1e-06
NEG = -1e30


def norm_rows(hidden, norm_gain):
    power = jnp.mean(hidden * hidden, axis=-1, keepdims=True)
    return (hidden * lax.rsqrt(power + EPS) * norm_gain).astype(jnp.bfloat16)


def expert_apply(tokens, gate, expert_in, expert_down):
    flat = tokens.reshape(-1, tokens.shape[-1])
    dims = (((1,), (1,)), ((), ()))
    gate_act = lax.dot_general(
        flat, expert_in[0, :, 0, :], dims, preferred_element_type=jnp.float32
    )
    up_act = lax.dot_general(flat, expert_in[0, :, 1, :], dims, preferred_element_type=jnp.float32)
    units = (jax.nn.silu(gate_act) * up_act).astype(jnp.bfloat16)
    part = jnp.dot(units, expert_down[0], preferred_element_type=jnp.float32)
    return (part * gate).astype(jnp.bfloat16)


def per_device(
    query_nope,
    query_rope,
    latent_new,
    key_rope,
    latent_pages,
    rope_pages,
    page_table,
    prefix_lengths,
    residual,
    key_up,
    value_up,
    out_weight,
    norm_gain,
    expert_in,
    expert_down,
    expert_ids,
    expert_weights,
):
    groups = lax.axis_size("dp")
    experts_all = lax.axis_size("expert") * expert_in.shape[0]
    tokens_col = query_nope.shape[1]
    block_rows = tokens_col // groups
    heads_here = key_up.shape[0]
    pages_lat, pages_rope = (
        lax.all_gather(latent_pages[0], "dp", axis=0, tiled=True),
        lax.all_gather(rope_pages[0], "dp", axis=0, tiled=True),
    )
    page_count = pages_lat.shape[0]
    table = page_table[0]
    inverse = jnp.sum(
        jnp.where(
            table[:, None] == jnp.arange(page_count)[None, :], jnp.arange(page_count)[:, None], 0
        ),
        axis=0,
    )
    positions = (inverse[:, None] * PAGE + jnp.arange(PAGE)[None, :]).reshape(-1)
    prefix_ok = positions < prefix_lengths[0]
    keys_lat = jnp.concatenate([pages_lat.reshape(-1, LAT), latent_new[0]], axis=0)
    keys_rope = jnp.concatenate([pages_rope.reshape(-1, RD), key_rope[0]], axis=0)
    heads_nope = query_nope[0].reshape(tokens_col, heads_here, HD)
    query_lat = jnp.einsum(
        "thd,hdc->thc", heads_nope, key_up, preferred_element_type=jnp.float32
    ).astype(jnp.bfloat16)
    heads_rope = query_rope[0].reshape(tokens_col, heads_here, RD)
    scale = 1.0 / (HD + RD) ** 0.5
    scores = (
        jnp.einsum("thc,kc->thk", query_lat, keys_lat, preferred_element_type=jnp.float32)
        + jnp.einsum("thr,kr->thk", heads_rope, keys_rope, preferred_element_type=jnp.float32)
    ) * scale
    causal = jnp.arange(tokens_col)[None, :] <= jnp.arange(tokens_col)[:, None]
    allowed = jnp.concatenate(
        [jnp.broadcast_to(prefix_ok[None, :], (tokens_col, prefix_ok.shape[0])), causal], axis=1
    )[:, None, :]
    masked = jnp.where(allowed, scores, NEG)
    peak = jnp.max(masked, axis=-1, keepdims=True)
    expo = jnp.where(allowed, jnp.exp(masked - peak), 0.0)
    total = jnp.sum(expo, axis=-1, keepdims=True)
    probs = expo.astype(jnp.bfloat16)
    attn_latent = (
        jnp.einsum("thk,kc->thc", probs, keys_lat, preferred_element_type=jnp.float32) / total
    ).astype(jnp.bfloat16)
    heads_out = jnp.einsum(
        "thc,hcd->thd", attn_latent, value_up, preferred_element_type=jnp.float32
    ).astype(jnp.bfloat16)
    partial_out = jnp.dot(
        heads_out.reshape(tokens_col, heads_here * HD),
        out_weight,
        preferred_element_type=jnp.float32,
    )
    attended = lax.psum_scatter(
        partial_out.astype(jnp.bfloat16), "dp", scatter_dimension=0, tiled=True
    ).astype(jnp.float32)
    start = lax.axis_index("dp") * block_rows
    hidden_mine = (
        lax.dynamic_slice_in_dim(residual[0], start, block_rows, 0).astype(jnp.float32) + attended
    )
    normed = norm_rows(hidden_mine, norm_gain)
    everyone = lax.all_gather(normed, ("expert", "dp"), axis=0, tiled=True)
    gates = jnp.sum(
        jnp.where(
            expert_ids[0][:, :, None] == jnp.arange(experts_all)[None, None, :],
            expert_weights[0][:, :, None],
            0.0,
        ),
        axis=1,
    )
    all_gates = lax.all_gather(gates, "expert", axis=0, tiled=True)
    mine = lax.axis_index("expert")
    gate = jnp.sum(
        jnp.where(jnp.arange(experts_all)[None, :] == mine, all_gates, 0.0), axis=1, keepdims=True
    )
    part = expert_apply(everyone, gate, expert_in, expert_down)
    mixture = lax.psum_scatter(
        part, ("expert", "dp"), scatter_dimension=0, tiled=True
    ).astype(jnp.float32)
    layer_out = (hidden_mine + mixture).astype(jnp.bfloat16)[None]
    return (layer_out, mixture.astype(jnp.bfloat16)[None])


def solution(mesh):
    return jax.shard_map(
        per_device,
        mesh=mesh,
        in_specs=(
            P("expert", None, "dp"),
            P("expert", None, "dp"),
            P("expert", None, None),
            P("expert", None, None),
            P("expert", "dp", None, None),
            P("expert", "dp", None),
            P("expert", None),
            P("expert"),
            P("expert", None, None),
            P("dp", None, None),
            P("dp", None, None),
            P("dp", None),
            P(),
            P("expert", "dp", None, None),
            P("expert", "dp", None),
            P("expert", None, None),
            P("expert", None, None),
        ),
        out_specs=(P("expert", "dp", None), P("expert", "dp", None)),
        check_vma=False,
    )
```

```python
import jax
import jax.numpy as jnp
from jax import lax
from jax.experimental import pallas as pl
from jax.experimental.pallas import tpu as pltpu
from jax.sharding import PartitionSpec as P

HD = 128
RD = 64
LAT = 512
TOP = 6
PAGE = 64


EPS = 1e-06
NEG = -1e30


def norm_rows(hidden, norm_gain):
    power = jnp.mean(hidden * hidden, axis=-1, keepdims=True)
    return (hidden * lax.rsqrt(power + EPS) * norm_gain).astype(jnp.bfloat16)


def expert_apply(tokens, gate, expert_in, expert_down):
    flat = tokens.reshape(-1, tokens.shape[-1])
    dims = (((1,), (1,)), ((), ()))
    gate_act = lax.dot_general(
        flat, expert_in[0, :, 0, :], dims, preferred_element_type=jnp.float32
    )
    up_act = lax.dot_general(flat, expert_in[0, :, 1, :], dims, preferred_element_type=jnp.float32)
    units = (jax.nn.silu(gate_act) * up_act).astype(jnp.bfloat16)
    part = jnp.dot(units, expert_down[0], preferred_element_type=jnp.float32)
    return (part * gate).astype(jnp.bfloat16)


def scatter_kernel(
    in_ref, out_ref, core_in, acc, diag_x, diag_y, from_x, from_y, z_send, z_up, z_down, sends, recvs
):
    x = lax.axis_index("dp")
    e = lax.axis_index("expert")
    z, y, c = e // 4, (e // 2) % 2, e % 2
    half = in_ref.shape[4] // 2
    high = z // 2
    low_z = z + high * (3 - 2 * z)
    order = [f + high * (3 - 2 * f) for f in (3 + 0 * z, 2 - 2 * low_z, 1 + low_z, low_z)]
    other_core = {"expert": e + 1 - 2 * c}
    other_y = {"expert": e + 2 - 4 * y}
    other_x = {"dp": 1 - x}
    above, below = {"expert": e + 4}, {"expert": e - 4}

    def copy(src, dst, kind, k, to):
        return pltpu.make_async_remote_copy(
            src_ref=src,
            dst_ref=dst,
            send_sem=sends.at[kind, k],
            recv_sem=recvs.at[kind, k],
            device_id=to,
            device_id_type=pl.DeviceIdType.MESH,
        )

    def core_copy(k):
        return copy(in_ref.at[order[k], :, 1 - c], core_in.at[k], 0, k, other_core)

    def diag_y_copy(k):
        return copy(acc.at[k, 1 - y, 1 - x, pl.ds(0, half)], diag_y.at[k], 1, k, other_y)

    def diag_x_copy(k):
        return copy(acc.at[k, 1 - y, 1 - x, pl.ds(half, half)], diag_x.at[k], 2, k, other_x)

    def x_copy(k):
        return copy(acc.at[k, y, 1 - x], from_x.at[k], 3, k, other_x)

    def y_copy(k):
        return copy(acc.at[k, 1 - y, x], from_y.at[k], 4, k, other_y)

    def up_copy(k):
        return copy(z_send.at[order[k]], z_up.at[order[k]], 5, order[k], above)

    def down_copy(k):
        return copy(z_send.at[order[k]], z_down.at[order[k]], 6, order[k], below)

    def wide(value):
        return value.astype(jnp.float32)

    barrier = pltpu.get_barrier_semaphore()
    for to in (other_core, other_x, other_y):
        pl.semaphore_signal(barrier, inc=1, device_id=to, device_id_type=pl.DeviceIdType.MESH)

    @pl.when(z > 0)
    def _():
        pl.semaphore_signal(barrier, inc=1, device_id=below, device_id_type=pl.DeviceIdType.MESH)

    @pl.when(z < 3)
    def _():
        pl.semaphore_signal(barrier, inc=1, device_id=above, device_id_type=pl.DeviceIdType.MESH)

    pl.semaphore_wait(barrier, 4 + ((z + 1) // 2) % 2)

    for k in range(4):
        core_copy(k).start()

    def stage_a(k):
        core_copy(k).wait_recv()
        for j in (0, 1):
            for i in (0, 1):
                acc[k, j, i] = (wide(in_ref[order[k], j, c, i]) + wide(core_in[k, j, i])).astype(
                    acc.dtype
                )
        diag_y_copy(k).start()
        diag_x_copy(k).start()

    def stage_b(k):
        top, bottom = pl.ds(0, half), pl.ds(half, half)
        diag_y_copy(k).wait_recv()
        acc[k, y, 1 - x, top] = (wide(acc[k, y, 1 - x, top]) + wide(diag_y[k])).astype(acc.dtype)
        x_copy(k).start()
        diag_x_copy(k).wait_recv()
        acc[k, 1 - y, x, bottom] = (wide(acc[k, 1 - y, x, bottom]) + wide(diag_x[k])).astype(
            acc.dtype
        )
        y_copy(k).start()

    def stage_c(k):
        x_copy(k).wait_recv()
        y_copy(k).wait_recv()
        g = order[k]
        out_ref[...] = wide(acc[k, y, x]) + wide(from_x[k]) + wide(from_y[k])

        @pl.when((g >= z) & (z > 0))
        def _():
            up_copy(k).wait_recv()
            out_ref[...] += wide(z_up[g])

        @pl.when((g <= z) & (z < 3))
        def _():
            down_copy(k).wait_recv()
            out_ref[...] += wide(z_down[g])

        if k < 3:
            z_send[g] = out_ref[...].astype(z_send.dtype)

            @pl.when(g > z)
            def _():
                up_copy(k).start()

            @pl.when(g < z)
            def _():
                down_copy(k).start()

    stage_a(0)
    stage_a(1)
    stage_b(0)
    stage_a(2)
    stage_b(1)
    stage_c(0)
    stage_a(3)
    stage_b(2)
    stage_c(1)
    stage_b(3)
    stage_c(2)
    stage_c(3)
    for k in range(4):
        for made in (core_copy, diag_y_copy, diag_x_copy, x_copy, y_copy):
            made(k).wait_send()
        if k < 3:

            @pl.when(order[k] > z)
            def _():
                up_copy(k).wait_send()

            @pl.when(order[k] < z)
            def _():
                down_copy(k).wait_send()


def scatter_sum(part):
    if lax.axis_size("dp") != 2 or lax.axis_size("expert") != 16:
        return lax.psum_scatter(
            part, ("expert", "dp"), scatter_dimension=0, tiled=True
        ).astype(jnp.float32)
    rows, width = part.shape[0] // 32, part.shape[1]
    kind = part.dtype
    return pl.pallas_call(
        scatter_kernel,
        out_shape=jax.ShapeDtypeStruct((rows, width), jnp.float32),
        in_specs=[pl.BlockSpec(memory_space=pltpu.VMEM)],
        out_specs=pl.BlockSpec(memory_space=pltpu.VMEM),
        scratch_shapes=[
            pltpu.VMEM((4, 2, 2, rows, width), kind),
            pltpu.VMEM((4, 2, 2, rows, width), kind),
            pltpu.VMEM((4, rows // 2, width), kind),
            pltpu.VMEM((4, rows // 2, width), kind),
            pltpu.VMEM((4, rows, width), kind),
            pltpu.VMEM((4, rows, width), kind),
            pltpu.VMEM((4, rows, width), kind),
            pltpu.VMEM((4, rows, width), kind),
            pltpu.VMEM((4, rows, width), kind),
            pltpu.SemaphoreType.DMA((7, 4)),
            pltpu.SemaphoreType.DMA((7, 4)),
        ],
        compiler_params=pltpu.CompilerParams(
            collective_id=0, has_side_effects=True, vmem_limit_bytes=48 * 2**20
        ),
    )(part.reshape(4, 2, 2, 2, rows, width))


def per_device(
    query_nope,
    query_rope,
    latent_new,
    key_rope,
    latent_pages,
    rope_pages,
    page_table,
    prefix_lengths,
    residual,
    key_up,
    value_up,
    out_weight,
    norm_gain,
    expert_in,
    expert_down,
    expert_ids,
    expert_weights,
):
    groups = lax.axis_size("dp")
    experts_all = lax.axis_size("expert") * expert_in.shape[0]
    tokens_col = query_nope.shape[1]
    block_rows = tokens_col // groups
    heads_here = key_up.shape[0]
    pages_lat, pages_rope = (
        lax.all_gather(latent_pages[0], "dp", axis=0, tiled=True),
        lax.all_gather(rope_pages[0], "dp", axis=0, tiled=True),
    )
    page_count = pages_lat.shape[0]
    table = page_table[0]
    inverse = jnp.sum(
        jnp.where(
            table[:, None] == jnp.arange(page_count)[None, :], jnp.arange(page_count)[:, None], 0
        ),
        axis=0,
    )
    positions = (inverse[:, None] * PAGE + jnp.arange(PAGE)[None, :]).reshape(-1)
    prefix_ok = positions < prefix_lengths[0]
    keys_lat = jnp.concatenate([pages_lat.reshape(-1, LAT), latent_new[0]], axis=0)
    keys_rope = jnp.concatenate([pages_rope.reshape(-1, RD), key_rope[0]], axis=0)
    heads_nope = query_nope[0].reshape(tokens_col, heads_here, HD)
    query_lat = jnp.einsum(
        "thd,hdc->thc", heads_nope, key_up, preferred_element_type=jnp.float32
    ).astype(jnp.bfloat16)
    heads_rope = query_rope[0].reshape(tokens_col, heads_here, RD)
    scale = 1.0 / (HD + RD) ** 0.5
    scores = (
        jnp.einsum("thc,kc->thk", query_lat, keys_lat, preferred_element_type=jnp.float32)
        + jnp.einsum("thr,kr->thk", heads_rope, keys_rope, preferred_element_type=jnp.float32)
    ) * scale
    causal = jnp.arange(tokens_col)[None, :] <= jnp.arange(tokens_col)[:, None]
    allowed = jnp.concatenate(
        [jnp.broadcast_to(prefix_ok[None, :], (tokens_col, prefix_ok.shape[0])), causal], axis=1
    )[:, None, :]
    masked = jnp.where(allowed, scores, NEG)
    peak = jnp.max(masked, axis=-1, keepdims=True)
    expo = jnp.where(allowed, jnp.exp(masked - peak), 0.0)
    total = jnp.sum(expo, axis=-1, keepdims=True)
    probs = expo.astype(jnp.bfloat16)
    attn_latent = (
        jnp.einsum("thk,kc->thc", probs, keys_lat, preferred_element_type=jnp.float32) / total
    ).astype(jnp.bfloat16)
    heads_out = jnp.einsum(
        "thc,hcd->thd", attn_latent, value_up, preferred_element_type=jnp.float32
    ).astype(jnp.bfloat16)
    partial_out = jnp.dot(
        heads_out.reshape(tokens_col, heads_here * HD),
        out_weight,
        preferred_element_type=jnp.float32,
    )
    attended = lax.psum_scatter(
        partial_out.astype(jnp.bfloat16), "dp", scatter_dimension=0, tiled=True
    ).astype(jnp.float32)
    start = lax.axis_index("dp") * block_rows
    hidden_mine = (
        lax.dynamic_slice_in_dim(residual[0], start, block_rows, 0).astype(jnp.float32) + attended
    )
    normed = norm_rows(hidden_mine, norm_gain)
    ids_mine = lax.dynamic_slice_in_dim(expert_ids[0], start, block_rows, 0)
    weights_mine = lax.dynamic_slice_in_dim(expert_weights[0], start, block_rows, 0)
    gates = jnp.sum(
        jnp.where(
            ids_mine[:, :, None] == jnp.arange(experts_all)[None, None, :],
            weights_mine[:, :, None],
            0.0,
        ),
        axis=1,
    )
    gates_high = gates.astype(jnp.bfloat16)
    gates_low = (gates - gates_high.astype(jnp.float32)).astype(jnp.bfloat16)
    model = normed.shape[1]
    extra = -(-2 * experts_all // 128) * 128
    fill = jnp.zeros((block_rows, extra - 2 * experts_all), jnp.bfloat16)
    sent = jnp.concatenate([normed, gates_high, gates_low, fill], axis=1)
    gathered = lax.all_gather(sent, ("expert", "dp"), axis=0, tiled=True)
    everyone = gathered[:, :model]
    mine = lax.axis_index("expert")
    named = (jnp.arange(extra) == mine) | (jnp.arange(extra) == mine + experts_all)
    gate = jnp.sum(
        jnp.where(named[None, :], gathered[:, model:].astype(jnp.float32), 0.0),
        axis=1,
        keepdims=True,
    )
    part = expert_apply(everyone, gate, expert_in, expert_down)
    mixture = scatter_sum(part)
    layer_out = (hidden_mine + mixture).astype(jnp.bfloat16)[None]
    return (layer_out, mixture.astype(jnp.bfloat16)[None])


def solution(mesh):
    return jax.shard_map(
        per_device,
        mesh=mesh,
        in_specs=(
            P("expert", None, "dp"),
            P("expert", None, "dp"),
            P("expert", None, None),
            P("expert", None, None),
            P("expert", "dp", None, None),
            P("expert", "dp", None),
            P("expert", None),
            P("expert"),
            P("expert", None, None),
            P("dp", None, None),
            P("dp", None, None),
            P("dp", None),
            P(),
            P("expert", "dp", None, None),
            P("expert", "dp", None),
            P("expert", None, None),
            P("expert", None, None),
        ),
        out_specs=(P("expert", "dp", None), P("expert", "dp", None)),
        check_vma=False,
    )
```
